32 devices in a mesh: expert: 16 (over z, y, x), dp: 2 (over core).
Axes of the slice: x: 2, y: 2, z: 4, core: 2. Of those that a mesh axis runs over, the one named last changes fastest.
Arguments:
- pooled: bfloat16 [8192, 256], P(('expert', 'dp')), may hold values from -6 to 6
- routes: int32 [8192, 2], P(('expert', 'dp')), may hold values from 0 to 15, all different within a row; in each aligned block of 256 rows (0 to 255, 256 to 511, ...) at most 48 rows name the same one
- labels: int32 [8192, 2], P(('expert', 'dp')), may hold values from 0 to 1
- in_weight: bfloat16 [16, 4096, 256], P('expert'), may hold values from -0.375 to 0.375
- out_weight: bfloat16 [16, 4096, 256], P('expert'), may hold values from -0.09375 to 0.09375
- gate_weight: bfloat16 [16, 2, 256], replicated, may hold values from -0.375 to 0.375
- tower_weight: float32 [2, 256], replicated, may hold values from -0.375 to 0.375
- tower_bias: float32 [2], replicated, may hold values from -3 to 3
- bag_rows: int32 [16384], P(('expert', 'dp')), may hold values from 0 to 1023
- bag_sample: int32 [16384], P(('expert', 'dp')), may hold values from 0 to 255
- bag_weight: float32 [16384], P(('expert', 'dp')), may hold values from 0.5 to 2
- row_table: float32 [16384, 256], P('expert'), may hold values from -6 to 6
Outputs:
- in_grad: float32 [16, 4096, 256], P('expert', 'dp')
- out_grad: float32 [16, 4096, 256], P('expert', 'dp')
- gate_grad: float32 [16, 2, 256], P('expert')
- tower_grad: float32 [2, 256], replicated
- new_table: float32 [16384, 256], P('expert')
The draws below stay inside these ranges and needn't reach their ends.
Inputs may be any that keep to these rules, and one draw needn't show every extreme that they name: `routes`: within each device's 256 rows no expert is named more than 48 times, a bound that some block reaches; a row's two experts differ.
All inputs are finite; a program needn't handle non-finite values.
Results may differ from the reference program's by a relative error of at most 0.0041.
Values may be sent and summed in bfloat16 or wider, within the bound.
A program may use at most 128 MiB of HBM per device.

```python
import math
import jax
import jax.numpy as jnp
import numpy as np
from jax import lax

FEAT = 256
HIDDEN_SIZE = 4096
TASKS = 2
TOK_DEV = 256
BAG_DEV = 512
TROWS_DEV = 1024
EXPERTS = 16
CAP = 48
PER_OWNER = 32
TOKENS = 8192
BAG_ALL = 16384
TROWS_ALL = 16384
N_EXPERT = 16
N_DP = 2


def place_ends(values, stream_key, low, top_value):
    index_at = [jax.random.randint(jax.random.fold_in(stream_key, axis), (), 0, length) for axis, length in enumerate(values.shape)]
    widest = values.shape.index(max(values.shape))
    beside = index_at[:widest] + [(index_at[widest] + 1) % values.shape[widest]] + index_at[widest + 1:]
    return values.at[tuple(index_at)].set(low).at[tuple(beside)].set(top_value)


def block_levels(stream_key, dims, split, low, high):
    gain, own = 1.0, jax.random.fold_in(stream_key, 6)
    for position, shards_of in split:
        steps = jnp.exp(jax.random.uniform(jax.random.fold_in(own, position), (shards_of,), jnp.float32, low / len(split), high / len(split)))
        gain = gain * jnp.repeat(steps, dims[position] // shards_of).reshape([-1 if axis == position else 1 for axis in range(len(dims))])
    return gain


def assign_block(rng, own, number, rows, number_of, top, limit, skew):
    order = jax.random.permutation(rng, number_of)
    crowded, ordinary = load_shares(number_of, rows * top, limit, skew, True), load_shares(number_of, rows * top, limit, skew, False)
    places = jnp.arange(number_of)

    def named(tallies, rotation):
        used = int((tallies > 0).sum())
        fixed = max(1, used // 4)
        shifted = fixed + (places - fixed + rotation * (used - fixed)) % max(1, number_of - fixed)
        return jnp.zeros((number_of,), jnp.int32).at[order[jnp.where(places < fixed, places, shifted)]].set(jnp.asarray(tallies, jnp.int32))

    tallies = jnp.where(number % 4 == 0, named(crowded, number // 4), named(ordinary, number - number // 4 - 1))
    mixed = jax.random.permutation(jax.random.fold_in(own, 3), number_of)
    giver, sink = mixed[0:number_of // 2 * 2:2], mixed[1:number_of // 2 * 2:2]
    room = jnp.minimum(tallies[giver] - 1, limit - tallies[sink]) // 2
    room = jnp.where((giver == order[0]) | (sink == order[0]) | (tallies[sink] == 0), 0, jnp.maximum(room, 0))
    shifted = jax.random.randint(jax.random.fold_in(own, 4), (number_of // 2,), 0, 1 << 20) % (room + 1)
    tallies = tallies.at[giver].add(-shifted).at[sink].add(shifted)
    items = jnp.searchsorted(jnp.cumsum(tallies), jnp.arange(rows * top), side="right").astype(jnp.int32)
    listing = items.reshape(top, rows).T
    listing = listing[jax.random.permutation(jax.random.fold_in(own, 1), rows)]
    rotation = jax.random.randint(jax.random.fold_in(own, 2), (rows, 1), 0, top)
    return jnp.take_along_axis(listing, (jnp.arange(top)[None, :] + rotation) % top, axis=1)


def load_shares(count, total, bound, lean, full):
    portions = [(1 << 20) // math.isqrt(grade ** lean) + 1 for grade in range(1, count + 1)]
    largest = bound if full else min(bound, max(-(-total // count), total * portions[0] // sum(portions)))
    least = 1 if total - largest >= count - 1 else 0
    given, spare = [largest] + [least] * (count - 1), total - largest - least * (count - 1)
    while spare > 0:
        candidates = [i for i in range(1, count) if given[i] < largest] or [i for i in range(1, count) if given[i] < bound]
        pool, budget = sum([portions[i] for i in candidates]), spare
        for i in candidates:
            more = min(bound - given[i], max(1, budget * portions[i] // pool), spare)
            given[i] = given[i] + more
            spare = spare - more
    return np.array(given)


def noise(own_key, shape, deviation, most, pieces=(), held_as=jnp.bfloat16):
    array = jax.random.normal(own_key, shape, jnp.float32) * deviation
    if len(pieces) > 0:
        array = block_levels(own_key, shape, pieces, -0.22, 0.18) * array
    return jnp.clip(array, min=-most, max=most).astype(held_as)


def setup_inputs(seed: int = 0) -> dict:
    arg_keys = jax.random.split(jax.random.key(seed), 13)
    pooled = noise(arg_keys[0], (TOKENS, FEAT), 1.0, 6.0, ((0, 32),))
    routes_keys = jax.random.split(jax.random.fold_in(arg_keys[1], 1), TOKENS // TOK_DEV)
    routes_turns = jax.random.permutation(jax.random.fold_in(arg_keys[1], 3), TOKENS // TOK_DEV)
    routes = jax.vmap(lambda own, number: assign_block(jax.random.fold_in(arg_keys[1], 2), own, number, TOK_DEV, EXPERTS, 2, CAP, 2))(routes_keys, routes_turns).reshape((TOKENS, 2))
    labels = place_ends(jax.random.randint(arg_keys[2], (TOKENS, TASKS), 0, 2), jax.random.fold_in(arg_keys[2], 1), 0, 1).astype(jnp.int32)
    in_weight = noise(arg_keys[3], (EXPERTS, HIDDEN_SIZE, FEAT), FEAT ** -0.5, 0.375, ((0, 16),))
    out_weight = noise(arg_keys[4], (EXPERTS, HIDDEN_SIZE, FEAT), HIDDEN_SIZE ** -0.5, 0.09375, ((0, 16),))
    gate_weight = noise(arg_keys[5], (EXPERTS, TASKS, FEAT), FEAT ** -0.5, 0.375)
    tower_weight = noise(arg_keys[6], (TASKS, FEAT), FEAT ** -0.5, 0.375, (), jnp.float32)
    tower_bias = noise(arg_keys[7], (TASKS,), 1.0, 3.0, (), jnp.float32)
    bag_rows = place_ends(jax.random.randint(arg_keys[8], (BAG_ALL,), 0, TROWS_DEV), jax.random.fold_in(arg_keys[8], 1), 0, TROWS_DEV - 1).astype(jnp.int32)
    bag_sample = place_ends(jax.random.randint(arg_keys[9], (BAG_ALL,), 0, TOK_DEV), jax.random.fold_in(arg_keys[9], 1), 0, TOK_DEV - 1).astype(jnp.int32)
    bag_weight = jnp.clip(jnp.exp(math.log(2.0) - 1.3862944 * jax.random.uniform(arg_keys[10], (BAG_ALL,), jnp.float32) ** block_levels(arg_keys[10], (BAG_ALL,), ((0, 32),), -0.2, 0.2)), 0.5, 2.0)
    row_table = noise(arg_keys[11], (TROWS_ALL, FEAT), 1.0, 6.0, ((0, 16),), jnp.float32)
    return {"pooled": pooled, "routes": routes, "labels": labels, "in_weight": in_weight, "out_weight": out_weight, "gate_weight": gate_weight, "tower_weight": tower_weight, "tower_bias": tower_bias, "bag_rows": bag_rows, "bag_sample": bag_sample, "bag_weight": bag_weight, "row_table": row_table}


LOSS_SCALE = 32.0
STEP_SIZE = 0.25
HIGH = lax.Precision.HIGHEST

def silu_grad(pre_silu):
    sigma = jax.nn.sigmoid(pre_silu)
    return sigma * (1.0 + pre_silu * (1.0 - sigma))

def reference(pooled, routes, labels, in_weight, out_weight, gate_weight, tower_weight, tower_bias, bag_rows, bag_sample, bag_weight, row_table):
    device_count = N_EXPERT * N_DP
    flat_routes = routes.reshape(device_count, TOK_DEV * 2)
    one_hot_int = (flat_routes[:, :, None] == jnp.arange(EXPERTS, dtype=jnp.int32)[None, None, :]).astype(jnp.int32)
    ranks = jnp.cumsum(one_hot_int, axis=1) - 1
    slot_of = lax.optimization_barrier(jnp.sum(ranks * one_hot_int, axis=2)).astype(jnp.int32)
    slot_index = (flat_routes * CAP + slot_of).astype(jnp.int32)

    def scatter_rows(values):
        empty = jnp.zeros((device_count, EXPERTS * CAP, FEAT), jnp.bfloat16)
        filled = jax.vmap(lambda buffer, where, rows_in: buffer.at[where].set(rows_in))(empty, slot_index, values)
        return filled.reshape(device_count, EXPERTS, CAP, FEAT).transpose(1, 0, 2, 3).reshape(EXPERTS, device_count * CAP, FEAT)

    def collect_rows(values):
        back = values.reshape(EXPERTS, device_count, CAP, FEAT).transpose(1, 0, 2, 3).reshape(device_count, EXPERTS * CAP, FEAT)
        picked = jax.vmap(lambda buffer, where: buffer[where])(back, slot_index)
        return picked.reshape(TOKENS, 2, FEAT)
    paired = jnp.repeat(pooled.reshape(device_count, TOK_DEV, FEAT), 2, axis=1)
    routed_in = scatter_rows(paired)

    def forward(items):
        inputs, in_matrix, out_matrix = items
        pre_silu = lax.dot_general(inputs, in_matrix, (((1,), (1,)), ((), ())), preferred_element_type=jnp.float32)
        hidden_act = jax.nn.silu(pre_silu).astype(jnp.bfloat16)
        return jnp.dot(hidden_act, out_matrix, preferred_element_type=jnp.float32).astype(jnp.bfloat16)
    expert_rows = lax.map(forward, (routed_in, in_weight, out_weight))
    expert_out = collect_rows(expert_rows).astype(jnp.float32)
    one_hot = (routes[:, :, None] == jnp.arange(EXPERTS, dtype=jnp.int32)[None, None, :]).astype(jnp.float32)
    gate_flat = gate_weight.reshape(EXPERTS * TASKS, FEAT)
    all_logits = lax.dot_general(pooled, gate_flat, (((1,), (1,)), ((), ())), preferred_element_type=jnp.float32).reshape(TOKENS, EXPERTS, TASKS)
    chosen = jnp.einsum('nke,net->ntk', one_hot, all_logits, precision=HIGH)
    gate_first = jax.nn.sigmoid(chosen[:, :, 0] - chosen[:, :, 1])
    gate_second = 1.0 - gate_first
    mixture = gate_first[:, :, None] * expert_out[:, None, 0, :] + gate_second[:, :, None] * expert_out[:, None, 1, :]
    task_logit = lax.optimization_barrier(jnp.sum(mixture * tower_weight[None], axis=2)) + tower_bias[None]
    logit_grad = LOSS_SCALE * (jax.nn.sigmoid(task_logit) - labels.astype(jnp.float32))
    tower_grad = jnp.einsum('nt,ntf->tf', logit_grad, mixture, precision=HIGH)
    mixture_grad = logit_grad[:, :, None] * tower_weight[None]
    routed_grad = jnp.stack([lax.optimization_barrier(jnp.sum(gate_first[:, :, None] * mixture_grad, axis=1)), lax.optimization_barrier(jnp.sum(gate_second[:, :, None] * mixture_grad, axis=1))], axis=1).astype(jnp.bfloat16)
    gate_dot = jnp.einsum('ntf,nkf->ntk', mixture_grad, expert_out, precision=HIGH)
    first_grad = (gate_dot[:, :, 0] - gate_dot[:, :, 1]) * gate_first * gate_second
    select_grad = jnp.stack([first_grad, -first_grad], axis=2)
    mix_table = jnp.einsum('nke,ntk->net', one_hot, select_grad, precision=HIGH).reshape(TOKENS, EXPERTS * TASKS)
    gate_grad = lax.dot_general(mix_table, pooled.astype(jnp.float32), (((0,), (0,)), ((), ())), precision=HIGH).reshape(EXPERTS, TASKS, FEAT)
    gate_input = jnp.dot(mix_table, gate_flat.astype(jnp.float32), precision=HIGH)
    routed_back = scatter_rows(routed_grad.reshape(device_count, TOK_DEV * 2, FEAT))

    def backward(items):
        inputs, grad_rows, in_matrix, out_matrix = items
        pre_silu = lax.dot_general(inputs, in_matrix, (((1,), (1,)), ((), ())), preferred_element_type=jnp.float32)
        hidden_act = jax.nn.silu(pre_silu).astype(jnp.bfloat16)
        hidden_grad = lax.dot_general(grad_rows, out_matrix, (((1,), (1,)), ((), ())), preferred_element_type=jnp.float32)
        pre_grad = (hidden_grad * silu_grad(pre_silu)).astype(jnp.bfloat16)
        in_part = lax.dot_general(pre_grad, inputs, (((0,), (0,)), ((), ())), preferred_element_type=jnp.float32)
        out_part = lax.dot_general(hidden_act, grad_rows, (((0,), (0,)), ((), ())), preferred_element_type=jnp.float32)
        input_grad = jnp.dot(pre_grad, in_matrix, preferred_element_type=jnp.float32).astype(jnp.bfloat16)
        return (in_part, out_part, input_grad)
    in_grad, out_grad, input_rows = lax.map(backward, (routed_in, routed_back, in_weight, out_weight))
    input_grad = collect_rows(input_rows).astype(jnp.float32)
    pooled_grad = gate_input + input_grad[:, 0] + input_grad[:, 1]
    entry = jnp.arange(BAG_ALL, dtype=jnp.int32)
    block_of = entry // BAG_DEV
    owner_of = entry % BAG_DEV // PER_OWNER
    sample_of = (block_of * TOK_DEV + bag_sample).astype(jnp.int32)
    row_grad = (bag_weight[:, None] * pooled_grad[sample_of]).astype(jnp.bfloat16)
    target = (owner_of * TROWS_DEV + bag_rows).astype(jnp.int32)
    row_sums = jax.ops.segment_sum(row_grad.astype(jnp.float32), target, num_segments=TROWS_ALL)
    new_table = row_table - STEP_SIZE * row_sums
    return (in_grad, out_grad, gate_grad, tower_grad, new_table)
```

```python
import jax
import jax.numpy as jnp
from jax import lax
from jax.sharding import PartitionSpec as P

LOSS_SCALE = 32.0
STEP_SIZE = 0.25
HIGH = lax.Precision.HIGHEST


def silu_grad(pre_silu):
    sigma = jax.nn.sigmoid(pre_silu)
    return sigma * (1.0 + pre_silu * (1.0 - sigma))


def contract_first(left, right):
    return lax.dot_general(
        left, right, (((0,), (0,)), ((), ())), preferred_element_type=jnp.float32
    )


def contract_last(left, right):
    return lax.dot_general(
        left, right, (((1,), (1,)), ((), ())), preferred_element_type=jnp.float32
    )


def on_device(
    pooled,
    routes,
    labels,
    in_weight,
    out_weight,
    gate_weight,
    tower_weight,
    tower_bias,
    bag_rows,
    bag_sample,
    bag_weight,
    row_table,
):
    owner_count = lax.axis_size("expert")
    tok_rows, feature = pooled.shape
    task_count = tower_weight.shape[0]
    capacity = 3 * tok_rows // owner_count
    in_matrix = in_weight[0]
    out_matrix = out_weight[0]
    experts = jnp.arange(owner_count, dtype=jnp.int32)[None, :]
    match_first = (routes[:, :1] == experts).astype(jnp.float32)
    match_second = (routes[:, 1:] == experts).astype(jnp.float32)
    before = jnp.tril(jnp.ones((tok_rows, tok_rows), jnp.float32), -1)
    ranks = jnp.dot(before, jnp.concatenate([match_first, match_second], axis=1))
    rank_first = ranks[:, :owner_count]
    rank_second = ranks[:, owner_count:] + jnp.sum(match_first, axis=0)[None]
    slot_first = jnp.sum(match_first * rank_first, axis=1).astype(jnp.int32) + routes[:, 0] * capacity
    slot_second = jnp.sum(match_second * rank_second, axis=1).astype(jnp.int32) + routes[:, 1] * capacity
    places = jnp.arange(owner_count * capacity, dtype=jnp.int32)[None, :]
    at_first = (slot_first[:, None] == places).astype(jnp.bfloat16)
    at_second = (slot_second[:, None] == places).astype(jnp.bfloat16)
    at_both = at_first + at_second

    def swap(values):
        return lax.all_to_all(values, "expert", split_axis=0, concat_axis=0, tiled=True)

    outbound = contract_first(at_both, pooled).astype(jnp.bfloat16)
    inputs = swap(outbound.reshape(owner_count, capacity, feature)).reshape(-1, feature)
    tower_out = lax.dot_general(
        tower_weight, out_matrix.astype(jnp.float32), (((1,), (1,)), ((), ())), precision=HIGH
    )
    pre_silu = contract_last(inputs, in_matrix)
    hidden_act = jax.nn.silu(pre_silu).astype(jnp.bfloat16)
    hidden_f32 = hidden_act.astype(jnp.float32)
    dots = lax.dot_general(
        tower_out, hidden_f32, (((1,), (1,)), ((), ())), precision=lax.Precision.HIGH
    )
    dots = dots.reshape(task_count, owner_count, capacity).transpose(1, 0, 2)
    dots = swap(dots).transpose(1, 0, 2).reshape(task_count, -1)
    dot_first = lax.dot_general(at_first.astype(jnp.float32), dots, (((1,), (1,)), ((), ())), precision=HIGH)
    dot_second = lax.dot_general(at_second.astype(jnp.float32), dots, (((1,), (1,)), ((), ())), precision=HIGH)
    gate_flat = gate_weight.reshape(-1, feature)
    all_logits = contract_last(pooled, gate_flat).reshape(tok_rows, owner_count, task_count)
    gate_first = jax.nn.sigmoid(
        jnp.sum((match_first - match_second)[:, :, None] * all_logits, axis=1)
    )
    gate_second = 1.0 - gate_first
    task_logit = gate_first * dot_first + gate_second * dot_second + tower_bias[None]
    logit_grad = LOSS_SCALE * (jax.nn.sigmoid(task_logit) - labels.astype(jnp.float32))
    first_grad = logit_grad * (dot_first - dot_second) * gate_first * gate_second
    scalars_first = jnp.concatenate([gate_first * logit_grad, first_grad], axis=1)
    scalars_second = jnp.concatenate([gate_second * logit_grad, -first_grad], axis=1)
    sent = lax.dot_general(
        scalars_first, at_first.astype(jnp.float32), (((0,), (0,)), ((), ())), precision=HIGH
    ) + lax.dot_general(
        scalars_second, at_second.astype(jnp.float32), (((0,), (0,)), ((), ())), precision=HIGH
    )
    sent = sent.reshape(2 * task_count, owner_count, capacity).transpose(1, 0, 2)
    scalars = swap(sent).transpose(1, 0, 2).reshape(2 * task_count, -1)
    coefs = scalars[:task_count]
    hidden_grad = sum(coefs[t][:, None] * tower_out[t][None, :] for t in range(task_count))
    pre_grad = (hidden_grad * silu_grad(pre_silu)).astype(jnp.bfloat16)
    input_rows = jnp.dot(pre_grad, in_matrix, preferred_element_type=jnp.float32).astype(jnp.bfloat16)
    mix_table = (
        (match_first - match_second)[:, :, None] * first_grad[:, None, :]
    ).reshape(tok_rows, owner_count * task_count)
    gate_input = jnp.dot(mix_table, gate_flat.astype(jnp.float32), precision=HIGH)
    back = swap(input_rows.reshape(owner_count, capacity, feature)).reshape(-1, feature)
    pooled_grad = gate_input + jnp.dot(at_both, back, preferred_element_type=jnp.float32)
    per_owner = bag_rows.shape[0] // owner_count
    row_grads = (bag_weight[:, None] * pooled_grad[bag_sample]).astype(jnp.bfloat16)
    owned_grads = swap(row_grads.reshape(owner_count, per_owner, feature))
    owned_rows = swap(bag_rows.reshape(owner_count, per_owner))
    hidden_sum = jnp.dot(coefs, hidden_f32, precision=lax.Precision.HIGH)
    in_grad = lax.psum_scatter(
        contract_first(pre_grad, inputs), "dp", scatter_dimension=0, tiled=True
    )
    gate_local = jnp.dot(scalars[task_count:], inputs.astype(jnp.float32), precision=HIGH)
    tower_local = jnp.dot(hidden_sum, out_matrix.astype(jnp.float32), precision=HIGH)
    tower_grad = lax.psum(tower_local, ("expert", "dp"))
    gate_grad = lax.psum(gate_local, "dp")
    hidden_mine = lax.psum_scatter(hidden_sum, "dp", scatter_dimension=1, tiled=True)
    out_grad = sum(hidden_mine[t][:, None] * tower_weight[t][None, :] for t in range(task_count))
    table_size = row_table.shape[0]
    matches = (
        owned_rows.reshape(-1)[:, None] == jnp.arange(table_size, dtype=jnp.int32)[None, :]
    ).astype(jnp.bfloat16)
    row_sums = lax.psum(contract_first(matches, owned_grads.reshape(-1, feature)), "dp")
    new_table = row_table - STEP_SIZE * row_sums
    return (in_grad[None], out_grad[None], gate_grad[None], tower_grad, new_table)


def solution(mesh):
    in_specs = (
        P(("expert", "dp"), None),
        P(("expert", "dp"), None),
        P(("expert", "dp"), None),
        P("expert", None, None),
        P("expert", None, None),
        P(),
        P(),
        P(),
        P(("expert", "dp")),
        P(("expert", "dp")),
        P(("expert", "dp")),
        P("expert", None),
    )
    out_specs = (
        P("expert", "dp", None),
        P("expert", "dp", None),
        P("expert", None, None),
        P(),
        P("expert", None),
    )
    return jax.shard_map(
        on_device, mesh=mesh, in_specs=in_specs, out_specs=out_specs, check_vma=False
    )
```

```python
import functools

import jax
import jax.numpy as jnp
from jax import lax
from jax.experimental import pallas as pl
from jax.experimental.pallas import tpu as pltpu
from jax.sharding import PartitionSpec as P

LOSS_SCALE = 32.0
STEP_SIZE = 0.25
F32, BF16 = jnp.float32, jnp.bfloat16
MESH = pl.DeviceIdType.MESH
VMEM_LIMIT = 62 * 2**20


def mm(left, right, left_dim=1, right_dim=0):
    return lax.dot_general(
        left, right, (((left_dim,), (right_dim,)), ((), ())), preferred_element_type=F32
    )


def nt(left, right):
    return mm(left, right, 1, 1)


def halves(value):
    high = value.astype(BF16).astype(F32)
    return high, value - high


def stacked(value):
    return jnp.concatenate(halves(value), axis=0).astype(BF16)


def folded(value):
    return value[:8] + value[8:]


def sigmoid(value):
    return 0.5 * jnp.tanh(0.5 * value) + 0.5


def iota(shape, dim):
    return lax.broadcasted_iota(jnp.int32, shape, dim)


def one_hot(condition):
    return jnp.where(condition, 1.0, 0.0)


def exchange(count, me, source, target, send_sem, recv_sem):
    def copy(peer, slot):
        return pltpu.make_async_remote_copy(
            src_ref=source.at[peer],
            dst_ref=target.at[slot],
            send_sem=send_sem.at[peer],
            recv_sem=recv_sem.at[slot],
            device_id={"expert": peer},
            device_id_type=MESH,
        )

    def start():
        @pl.loop(1, count)
        def _(step):
            copy(lax.rem(me + step, count), me).start()

        target[me] = source[me]

    def wait():
        @pl.loop(1, count)
        def _(step):
            peer = lax.rem(me + step, count)
            copy(peer, peer).wait_recv()

    def drain():
        @pl.loop(1, count)
        def _(step):
            copy(lax.rem(me + step, count), me).wait_send()

    return start, wait, drain


def kernel(
    sizes,
    pooled_ref,
    routes_ref,
    routes_rows_ref,
    labels_ref,
    in_hbm,
    out_hbm,
    gate_ref,
    tower_ref,
    bias_ref,
    bag_rows_ref,
    bag_sample_ref,
    bag_weight_ref,
    in_parts_ref,
    hidden_parts_ref,
    small_ref,
    grads_ref,
    rows_ref,
    in_ref,
    out_ref,
    turned_ref,
    proj_rows_ref,
    proj_cols_ref,
    act_ref,
    slope_ref,
    pre_ref,
    place_ref,
    a_send,
    a_recv,
    b_send,
    b_recv,
    c_send,
    c_recv,
    d_send,
    d_recv,
    e_send,
    e_recv,
    r_recv,
    t_send,
    t_recv,
    s_send,
    s_recv,
    in_other,
    hidden_other,
    rows_acc,
    back_acc,
    send_sem,
    recv_sem,
    dp_send,
    dp_recv,
    local_sem,
):
    count, cap, chunk, chunks = sizes
    rows_all = count * cap
    tok_rows = pooled_ref.shape[0]
    me, core = lax.axis_index("expert"), lax.axis_index("dp")
    other = 1 - core
    half = chunks // 2

    def phase(index, source, target):
        return exchange(count, me, source, target, send_sem.at[index], recv_sem.at[index])

    a_start, a_wait, a_drain = phase(0, a_send, a_recv)
    b_start, b_wait, b_drain = phase(1, b_send, b_recv)
    c_start, c_wait, c_drain = phase(2, c_send, c_recv)
    d_start, d_wait, d_drain = phase(3, d_send, d_recv)
    e_start, e_wait, e_drain = phase(4, e_send, e_recv)
    r_start, r_wait, r_drain = phase(5, bag_rows_ref, r_recv)
    t_start, t_wait, t_drain = phase(6, t_send, t_recv)

    def to_other(index, source, target):
        return pltpu.make_async_remote_copy(
            src_ref=source,
            dst_ref=target,
            send_sem=dp_send.at[index],
            recv_sem=dp_recv.at[index],
            device_id={"dp": other},
            device_id_type=MESH,
        )

    barrier = pltpu.get_barrier_semaphore()

    @pl.loop(1, count)
    def _(step):
        pl.semaphore_signal(
            barrier, inc=1, device_id={"expert": lax.rem(me + step, count)}, device_id_type=MESH
        )

    pl.semaphore_signal(barrier, inc=1, device_id={"dp": other}, device_id_type=MESH)
    load_out = pltpu.make_async_copy(out_hbm, out_ref, local_sem.at[0])
    load_in = pltpu.make_async_copy(in_hbm, in_ref, local_sem.at[1])
    load_out.start()
    load_in.start()

    first_row, second_row = routes_rows_ref[0:1, :], routes_rows_ref[1:2, :]
    first_map = one_hot(iota((count, tok_rows), 0) == first_row)
    second_map = one_hot(iota((count, tok_rows), 0) == second_row)
    above = one_hot(
        iota((tok_rows, tok_rows), 0) < iota((tok_rows, tok_rows), 1)
    ).astype(BF16)
    first_total = jnp.sum(first_map, axis=1, keepdims=True)
    first_rank = jnp.sum(first_map * mm(first_map.astype(BF16), above), axis=0, keepdims=True)
    second_rank = jnp.sum(
        second_map * (mm(second_map.astype(BF16), above) + first_total), axis=0, keepdims=True
    )
    first_slot = first_rank.astype(jnp.int32) + first_row * cap
    second_slot = second_rank.astype(jnp.int32) + second_row * cap
    places = iota((rows_all, tok_rows), 0)
    fill = one_hot((places == first_slot) | (places == second_slot)).astype(BF16)
    place_ref[...] = fill
    a_send[...] = mm(fill, pooled_ref[...]).astype(BF16).reshape(a_send.shape)
    pl.semaphore_wait(barrier, count)
    a_start()
    r_start()

    lanes = iota((128, tok_rows), 0)
    first_at = one_hot(lanes == first_rank.astype(jnp.int32)).astype(BF16)
    second_at = one_hot(lanes == second_rank.astype(jnp.int32)).astype(BF16)
    signed = first_map - second_map
    row_of = iota((8, tok_rows), 0)
    gate_logit = jnp.zeros((8, tok_rows), F32)
    for task in range(2):
        logits = nt(gate_ref[task], pooled_ref[...])
        gate_logit = jnp.where(
            row_of == task, jnp.sum(signed * logits, axis=0, keepdims=True), gate_logit
        )
    gate_first = sigmoid(gate_logit)
    gate_second = 1.0 - gate_first
    tower_high, tower_low = halves(tower_ref[...])
    tower_high, tower_low = tower_high.astype(BF16), tower_low.astype(BF16)
    load_out.wait()
    load_in.wait()

    @pl.loop(0, chunks)
    def _(step):
        span = pl.ds(pl.multiple_of(step * chunk, chunk), chunk)
        weights = out_ref[span, :]
        proj_rows_ref[step] = stacked(nt(tower_high, weights) + nt(tower_low, weights))
        proj_cols_ref[span, :] = nt(weights, tower_high) + nt(weights, tower_low)
        turned_ref[step] = in_ref[span, :].T

    a_wait()
    rows_acc[...] = jnp.zeros_like(rows_acc)

    @pl.loop(0, chunks)
    def _(step):
        span = pl.ds(pl.multiple_of(step * chunk, chunk), chunk)
        before = nt(in_ref[span, :], a_recv[...].reshape(rows_all, -1))
        sigma = sigmoid(before)
        act = before * sigma
        slope_ref[span, :] = (sigma + act * (1.0 - sigma)).astype(slope_ref.dtype)
        act = act.astype(BF16)
        act_ref[span, :] = act
        rows_acc[...] += mm(proj_rows_ref[step], act)

    dots = folded(rows_acc[...])

    @pl.loop(0, count)
    def _(peer):
        b_send[peer] = pltpu.roll(dots, lax.rem(rows_all - peer * cap, rows_all), 1)[:, :128]

    b_start()
    b_wait()
    owner_of = iota((count * 8, tok_rows), 0) // 8
    first_mask = one_hot(owner_of == first_row)
    second_mask = one_hot(owner_of == second_row)
    got_high, got_low = halves(
        jnp.where(iota((count * 8, 128), 1) < cap, b_recv[...].reshape(count * 8, 128), 0.0)
    )

    def pick(mask, where):
        found = mm(got_high.astype(BF16), where) + mm(got_low.astype(BF16), where)
        return jnp.sum((mask * found).reshape(count, 8, tok_rows), axis=0)

    first_dot, second_dot = pick(first_mask, first_at), pick(second_mask, second_at)
    task_logit = gate_first * first_dot + gate_second * second_dot + bias_ref[...]
    logit_grad = LOSS_SCALE * (sigmoid(task_logit) - labels_ref[...])
    first_grad = logit_grad * (first_dot - second_dot) * gate_first * gate_second
    lower = pltpu.roll(first_grad, 2, 0)
    keep = row_of < 4
    first_vals = jnp.where(keep, jnp.where(row_of < 2, gate_first * logit_grad, lower), 0.0)
    second_vals = jnp.where(keep, jnp.where(row_of < 2, gate_second * logit_grad, -lower), 0.0)

    def spread(vals, mask, where):
        wide = jnp.broadcast_to(vals[None], (count, 8, tok_rows)).reshape(count * 8, tok_rows)
        high, low = halves(wide * mask)
        return nt(high.astype(BF16), where) + nt(low.astype(BF16), where)

    c_send[...] = (
        spread(first_vals, first_mask, first_at) + spread(second_vals, second_mask, second_at)
    ).reshape(c_send.shape)
    c_start()
    gate_input = jnp.zeros((tok_rows, pooled_ref.shape[1]), F32)
    for task in range(2):
        high, low = halves(signed * first_grad[task : task + 1, :])
        weights = gate_ref[task]
        gate_input += mm(high.astype(BF16), weights, 0, 0) + mm(low.astype(BF16), weights, 0, 0)
    c_wait()
    coefs = jnp.zeros((8, rows_all), F32)
    blank = jnp.zeros((8, rows_all - 128), F32)

    def place(peer, total):
        return total + pltpu.roll(
            jnp.concatenate([c_recv[peer], blank], axis=1), peer * cap, 1
        )

    coefs = lax.fori_loop(0, count, place, coefs)
    coef_zero, coef_one = coefs[0:1, :], coefs[1:2, :]
    back_acc[...] = jnp.zeros_like(back_acc)

    @pl.loop(0, chunks)
    def _(step):
        span = pl.ds(pl.multiple_of(step * chunk, chunk), chunk)
        cols = proj_cols_ref[span, :]
        hidden_grad = cols[:, 0:1] * coef_zero + cols[:, 1:2] * coef_one
        grad = (hidden_grad * slope_ref[span, :].astype(F32)).astype(BF16)
        pre_ref[span, :] = grad
        back_acc[...] += mm(turned_ref[step], grad)

    d_send[...] = back_acc[...].T.astype(BF16).reshape(d_send.shape)
    d_start()

    coef_rows = stacked(coefs)

    def weight_chunk(step, in_target, hidden_target, slot):
        span = pl.ds(pl.multiple_of(step * chunk, chunk), chunk)
        in_target[pl.ds(pl.multiple_of(slot * chunk, chunk), chunk), :] = mm(
            pre_ref[span, :], a_recv[...].reshape(rows_all, -1)
        )
        hidden = folded(nt(coef_rows, act_ref[span, :]))
        hidden_target[slot] = hidden
        return folded(mm(stacked(hidden), out_ref[span, :]))

    tower = jnp.zeros((8, pooled_ref.shape[1]), F32)
    tower = lax.fori_loop(
        0,
        half,
        lambda i, total: total + weight_chunk(other * half + i, in_other, hidden_other, i),
        tower,
    )
    in_copy = to_other(0, in_other, in_parts_ref.at[1])
    hidden_copy = to_other(1, hidden_other, hidden_parts_ref.at[1])
    in_copy.start()
    hidden_copy.start()
    d_wait()
    pooled_grad = gate_input + mm(
        place_ref[...], d_recv[...].reshape(rows_all, -1), 0, 0
    )
    bag = one_hot(iota((bag_sample_ref.shape[0], tok_rows), 1) == bag_sample_ref[...]).astype(BF16)
    high, low = halves(pooled_grad)
    bag_grad = mm(bag, high.astype(BF16)) + mm(bag, low.astype(BF16))
    e_send[...] = (bag_weight_ref[...] * bag_grad).astype(BF16).reshape(e_send.shape)
    e_start()
    tower = lax.fori_loop(
        0,
        half,
        lambda i, total: total
        + weight_chunk(core * half + i, in_parts_ref.at[0], hidden_parts_ref.at[0], i),
        tower,
    )
    gate = folded(mm(coef_rows, a_recv[...].reshape(rows_all, -1)))
    tile = jnp.where(iota(tower.shape, 0) < 2, tower, gate)
    t_send[...] = jnp.broadcast_to(tile[None], t_send.shape)
    t_start()
    r_wait()
    e_wait()
    grads_copy = to_other(2, e_recv, grads_ref.at[core])
    rows_copy = to_other(3, r_recv, rows_ref.at[core])
    grads_copy.start()
    rows_copy.start()
    grads_ref[core] = e_recv[...]
    rows_ref[core] = r_recv[...]
    t_wait()
    summed = lax.fori_loop(0, count, lambda i, total: total + t_recv[i], jnp.zeros_like(tower))
    mine = jnp.where(iota(tower.shape, 0) < 2, summed, tile)
    s_send[...] = mine
    small_copy = to_other(4, s_send, s_recv)
    small_copy.start()
    small_copy.wait()
    small_ref[...] = mine + s_recv[...]
    for copy in (in_copy, hidden_copy, grads_copy, rows_copy):
        copy.wait()
    for drain in (a_drain, b_drain, c_drain, d_drain, e_drain, r_drain, t_drain):
        drain()


def on_device(
    pooled,
    routes,
    labels,
    in_weight,
    out_weight,
    gate_weight,
    tower_weight,
    tower_bias,
    bag_rows,
    bag_sample,
    bag_weight,
    row_table,
):
    count = lax.axis_size("expert")
    tok_rows, feature = pooled.shape
    tasks = tower_weight.shape[0]
    hidden = in_weight.shape[1]
    cap = -(-(3 * tok_rows // count) // 8) * 8
    rows_all = count * cap
    chunk = 256
    chunks = hidden // chunk
    per_owner = bag_rows.shape[0] // count
    held = -(-per_owner // 8) * 8

    def bags(values, empty):
        return jnp.pad(
            values.reshape(count, per_owner), ((0, 0), (0, held - per_owner)), constant_values=empty
        )

    def rows8(values):
        return jnp.pad(values, ((0, 8 - values.shape[0]), (0, 0)))

    bag_tiles = jnp.pad(
        bag_rows.reshape(count, 1, per_owner), ((0, 0), (0, 7), (0, 128 - per_owner)), constant_values=-1
    )
    vmem = pl.BlockSpec(memory_space=pltpu.VMEM)
    anywhere = pl.BlockSpec(memory_space=pl.ANY)
    scalars = (count, 8, 128)
    routed = (count, cap, feature)
    owned = (count, held, feature)
    half_rows = hidden // 2
    in_parts, hidden_parts, small, grads, rows = pl.pallas_call(
        functools.partial(kernel, (count, cap, chunk, chunks)),
        out_shape=(
            jax.ShapeDtypeStruct((2, half_rows, feature), F32),
            jax.ShapeDtypeStruct((2, chunks // 2, 8, chunk), F32),
            jax.ShapeDtypeStruct((8, feature), F32),
            jax.ShapeDtypeStruct((2,) + owned, BF16),
            jax.ShapeDtypeStruct((2,) + scalars, jnp.int32),
        ),
        in_specs=[vmem] * 4 + [anywhere] * 2 + [vmem] * 6,
        out_specs=(vmem,) * 5,
        scratch_shapes=[
            pltpu.VMEM((hidden, feature), BF16),
            pltpu.VMEM((hidden, feature), BF16),
            pltpu.VMEM((chunks, feature, chunk), BF16),
            pltpu.VMEM((chunks, 16, chunk), BF16),
            pltpu.VMEM((hidden, 8), F32),
            pltpu.VMEM((hidden, rows_all), BF16),
            pltpu.VMEM((hidden, rows_all), F32),
            pltpu.VMEM((hidden, rows_all), BF16),
            pltpu.VMEM((rows_all, tok_rows), BF16),
            pltpu.VMEM(routed, BF16),
            pltpu.VMEM(routed, BF16),
            pltpu.VMEM(scalars, F32),
            pltpu.VMEM(scalars, F32),
            pltpu.VMEM(scalars, F32),
            pltpu.VMEM(scalars, F32),
            pltpu.VMEM(routed, BF16),
            pltpu.VMEM(routed, BF16),
            pltpu.VMEM(owned, BF16),
            pltpu.VMEM(owned, BF16),
            pltpu.VMEM(scalars, jnp.int32),
            pltpu.VMEM((count, 8, feature), F32),
            pltpu.VMEM((count, 8, feature), F32),
            pltpu.VMEM((8, feature), F32),
            pltpu.VMEM((8, feature), F32),
            pltpu.VMEM((half_rows, feature), F32),
            pltpu.VMEM((chunks // 2, 8, chunk), F32),
            pltpu.VMEM((16, rows_all), F32),
            pltpu.VMEM((feature, rows_all), F32),
            pltpu.SemaphoreType.DMA((7, count)),
            pltpu.SemaphoreType.DMA((7, count)),
            pltpu.SemaphoreType.DMA((5,)),
            pltpu.SemaphoreType.DMA((5,)),
            pltpu.SemaphoreType.DMA((2,)),
        ],
        compiler_params=pltpu.CompilerParams(
            collective_id=0, has_side_effects=True, vmem_limit_bytes=VMEM_LIMIT
        ),
    )(
        pooled,
        routes,
        rows8(routes.T),
        rows8(labels.T.astype(F32)),
        in_weight[0],
        out_weight[0],
        gate_weight.transpose(1, 0, 2),
        rows8(tower_weight),
        rows8(tower_bias[:, None]),
        bag_tiles,
        bags(bag_sample, -1).reshape(-1, 1),
        bags(bag_weight, 0.0).reshape(-1, 1),
    )
    in_grad = (in_parts[0] + in_parts[1])[None]
    hidden_sum = (hidden_parts[0] + hidden_parts[1])[:, :tasks, :]
    out_grad = sum(
        hidden_sum[:, t].reshape(-1, 1) * tower_weight[t][None, :] for t in range(tasks)
    )[None]
    owned_rows = rows[:, :, 0, :held].reshape(-1)
    matches = (
        jnp.arange(row_table.shape[0], dtype=jnp.int32)[:, None] == owned_rows[None, :]
    ).astype(BF16)
    new_table = row_table - STEP_SIZE * mm(matches, grads.reshape(-1, feature))
    return (in_grad, out_grad, small[None, tasks : 2 * tasks], small[:tasks], new_table)


def solution(mesh):
    in_specs = (
        P(("expert", "dp"), None),
        P(("expert", "dp"), None),
        P(("expert", "dp"), None),
        P("expert", None, None),
        P("expert", None, None),
        P(),
        P(),
        P(),
        P(("expert", "dp")),
        P(("expert", "dp")),
        P(("expert", "dp")),
        P("expert", None),
    )
    out_specs = (
        P("expert", "dp", None),
        P("expert", "dp", None),
        P("expert", None, None),
        P(),
        P("expert", None),
    )
    return jax.shard_map(
        on_device, mesh=mesh, in_specs=in_specs, out_specs=out_specs, check_vma=False
    )
```

```python
import functools

import jax
import jax.numpy as jnp
from jax import lax
from jax.experimental import pallas as pl
from jax.experimental.pallas import tpu as pltpu
from jax.sharding import PartitionSpec as P

LOSS_SCALE = 32.0
STEP_SIZE = 0.25
F32, BF16 = jnp.float32, jnp.bfloat16
MESH = pl.DeviceIdType.MESH
VMEM_LIMIT = 62 * 2**20


def mm(left, right, left_dim=1, right_dim=0):
    return lax.dot_general(
        left, right, (((left_dim,), (right_dim,)), ((), ())), preferred_element_type=F32
    )


def nt(left, right):
    return mm(left, right, 1, 1)


def halves(value):
    high = value.astype(BF16).astype(F32)
    return high, value - high


def stacked(value):
    return jnp.concatenate(halves(value), axis=0).astype(BF16)


def folded(value):
    return value[:8] + value[8:]


def sigmoid(value):
    return 0.5 * jnp.tanh(0.5 * value) + 0.5


def iota(shape, dim):
    return lax.broadcasted_iota(jnp.int32, shape, dim)


def one_hot(condition):
    return jnp.where(condition, 1.0, 0.0)


def exchange(count, me, source, target, send_sem, recv_sem):
    def copy(peer, slot):
        return pltpu.make_async_remote_copy(
            src_ref=source.at[peer],
            dst_ref=target.at[slot],
            send_sem=send_sem.at[peer],
            recv_sem=recv_sem.at[slot],
            device_id={"expert": peer},
            device_id_type=MESH,
        )

    def start():
        @pl.loop(1, count)
        def _(step):
            copy(lax.rem(me + step, count), me).start()

        target[me] = source[me]

    def wait():
        @pl.loop(1, count)
        def _(step):
            peer = lax.rem(me + step, count)
            copy(peer, peer).wait_recv()

    def drain():
        @pl.loop(1, count)
        def _(step):
            copy(lax.rem(me + step, count), me).wait_send()

    return start, wait, drain


def kernel(
    sizes,
    pooled_ref,
    routes_rows_ref,
    labels_ref,
    in_hbm,
    out_hbm,
    gate_ref,
    tower_ref,
    bias_ref,
    bag_rows_ref,
    bag_sample_ref,
    bag_weight_ref,
    in_mine_hbm,
    in_recv_hbm,
    hidden_parts_ref,
    small_ref,
    grads_ref,
    rows_ref,
    in_ref,
    out_ref,
    turned_ref,
    proj_rows_ref,
    proj_cols_ref,
    act_ref,
    slope_ref,
    pre_ref,
    place_ref,
    a_send,
    a_recv,
    b_send,
    b_recv,
    c_send,
    c_recv,
    d_send,
    d_recv,
    e_send,
    e_recv,
    r_send,
    r_recv,
    t_send,
    t_recv,
    s_send,
    s_recv,
    in_mine,
    in_other,
    hidden_other,
    rows_acc,
    back_acc,
    send_sem,
    recv_sem,
    dp_send,
    dp_recv,
    local_sem,
):
    count, cap, chunk, chunks, per_owner = sizes
    rows_all = count * cap
    tok_rows = pooled_ref.shape[0]
    me, core = lax.axis_index("expert"), lax.axis_index("dp")
    other = 1 - core
    half = chunks // 2

    def phase(index, source, target):
        return exchange(count, me, source, target, send_sem.at[index], recv_sem.at[index])

    a_start, a_wait, a_drain = phase(0, a_send, a_recv)
    b_start, b_wait, b_drain = phase(1, b_send, b_recv)
    c_start, c_wait, c_drain = phase(2, c_send, c_recv)
    d_start, d_wait, d_drain = phase(3, d_send, d_recv)
    e_start, e_wait, e_drain = phase(4, e_send, e_recv)
    r_start, r_wait, r_drain = phase(5, r_send, r_recv)
    t_start, t_wait, t_drain = phase(6, t_send, t_recv)

    def to_other(index, source, target):
        return pltpu.make_async_remote_copy(
            src_ref=source,
            dst_ref=target,
            send_sem=dp_send.at[index],
            recv_sem=dp_recv.at[index],
            device_id={"dp": other},
            device_id_type=MESH,
        )

    barrier = pltpu.get_barrier_semaphore()

    @pl.loop(1, count)
    def _(step):
        pl.semaphore_signal(
            barrier, inc=1, device_id={"expert": lax.rem(me + step, count)}, device_id_type=MESH
        )

    pl.semaphore_signal(barrier, inc=1, device_id={"dp": other}, device_id_type=MESH)
    load_out = pltpu.make_async_copy(out_hbm, out_ref, local_sem.at[0])
    load_in = pltpu.make_async_copy(in_hbm, in_ref, local_sem.at[1])
    load_out.start()
    load_in.start()

    first_row, second_row = routes_rows_ref[0:1, :], routes_rows_ref[1:2, :]
    first_map = one_hot(iota((count, tok_rows), 0) == first_row)
    second_map = one_hot(iota((count, tok_rows), 0) == second_row)
    above = one_hot(
        iota((tok_rows, tok_rows), 0) < iota((tok_rows, tok_rows), 1)
    ).astype(BF16)
    first_total = jnp.sum(first_map, axis=1, keepdims=True)
    first_rank = jnp.sum(first_map * mm(first_map.astype(BF16), above), axis=0, keepdims=True)
    second_rank = jnp.sum(
        second_map * (mm(second_map.astype(BF16), above) + first_total), axis=0, keepdims=True
    )
    first_slot = first_rank.astype(jnp.int32) + first_row * cap
    second_slot = second_rank.astype(jnp.int32) + second_row * cap
    places = iota((rows_all, tok_rows), 0)
    fill = one_hot((places == first_slot) | (places == second_slot)).astype(BF16)
    place_ref[...] = fill
    a_send[...] = mm(fill, pooled_ref[...]).astype(BF16).reshape(a_send.shape)

    @pl.loop(0, count)
    def _(owner):
        line = bag_rows_ref[pl.ds(owner * per_owner // 128, 1), :]
        shift = lax.rem(128 - lax.rem(owner * per_owner, 128), 128)
        line = pltpu.roll(jnp.broadcast_to(line, (8, 128)), shift, 1)
        r_send[owner] = jnp.where(iota((8, 128), 1) < per_owner, line, -1)

    pl.semaphore_wait(barrier, count)
    a_start()
    r_start()

    lanes = iota((128, tok_rows), 0)
    first_at = one_hot(lanes == first_rank.astype(jnp.int32)).astype(BF16)
    second_at = one_hot(lanes == second_rank.astype(jnp.int32)).astype(BF16)
    signed = first_map - second_map
    row_of = iota((8, tok_rows), 0)
    labels = jnp.where(row_of == 0, labels_ref[0:1, :], labels_ref[1:2, :]).astype(F32)
    bias = jnp.where(row_of == 0, bias_ref[0], bias_ref[1])
    gates = [gate_ref[:, task, :] for task in range(2)]
    feat_row = iota((8, tower_ref.shape[1]), 0)
    tower_rows = jnp.where(
        feat_row == 0, tower_ref[0:1, :], jnp.where(feat_row == 1, tower_ref[1:2, :], 0.0)
    )
    sample_wide = jnp.broadcast_to(bag_sample_ref[...].astype(F32), (8, bag_sample_ref.shape[1]))
    weight_wide = jnp.broadcast_to(bag_weight_ref[...], (8, bag_sample_ref.shape[1]))
    sample_col, weight_col = sample_wide.T[:, 0:1], weight_wide.T[:, 0:1]
    bag = one_hot(
        iota((bag_sample_ref.shape[1], tok_rows), 1) == sample_col.astype(jnp.int32)
    ).astype(BF16)
    gate_logit = jnp.zeros((8, tok_rows), F32)
    for task in range(2):
        logits = nt(gates[task], pooled_ref[...])
        gate_logit = jnp.where(
            row_of == task, jnp.sum(signed * logits, axis=0, keepdims=True), gate_logit
        )
    gate_first = sigmoid(gate_logit)
    gate_second = 1.0 - gate_first
    tower_high, tower_low = halves(tower_rows)
    tower_high, tower_low = tower_high.astype(BF16), tower_low.astype(BF16)
    load_out.wait()
    load_in.wait()

    @pl.loop(0, chunks)
    def _(step):
        span = pl.ds(pl.multiple_of(step * chunk, chunk), chunk)
        weights = out_ref[span, :]
        proj_rows_ref[step] = stacked(nt(tower_high, weights) + nt(tower_low, weights))
        proj_cols_ref[span, :] = nt(weights, tower_high) + nt(weights, tower_low)
        turned_ref[step] = in_ref[span, :].T

    a_wait()
    rows_acc[...] = jnp.zeros_like(rows_acc)

    @pl.loop(0, chunks)
    def _(step):
        span = pl.ds(pl.multiple_of(step * chunk, chunk), chunk)
        before = nt(in_ref[span, :], a_recv[...].reshape(rows_all, -1))
        near = 0.5 * before
        bend = jnp.tanh(near)
        bent = near * bend
        slope_ref[span, :] = (1.0 + bend) + (near - bent * bend)
        act = (near + bent).astype(BF16)
        act_ref[span, :] = act
        rows_acc[...] += mm(proj_rows_ref[step], act)

    dots = folded(rows_acc[...])

    @pl.loop(0, count)
    def _(peer):
        b_send[peer] = pltpu.roll(dots, lax.rem(rows_all - peer * cap, rows_all), 1)[:, :128]

    b_start()
    b_wait()
    owner_of = iota((count * 8, tok_rows), 0) // 8
    first_mask = one_hot(owner_of == first_row)
    second_mask = one_hot(owner_of == second_row)
    got_high, got_low = halves(
        jnp.where(iota((count * 8, 128), 1) < cap, b_recv[...].reshape(count * 8, 128), 0.0)
    )

    def pick(mask, where):
        found = mm(got_high.astype(BF16), where) + mm(got_low.astype(BF16), where)
        return jnp.sum((mask * found).reshape(count, 8, tok_rows), axis=0)

    first_dot, second_dot = pick(first_mask, first_at), pick(second_mask, second_at)
    task_logit = gate_first * first_dot + gate_second * second_dot + bias
    logit_grad = LOSS_SCALE * (sigmoid(task_logit) - labels)
    first_grad = logit_grad * (first_dot - second_dot) * gate_first * gate_second
    lower = pltpu.roll(first_grad, 2, 0)
    keep = row_of < 4
    first_vals = jnp.where(keep, jnp.where(row_of < 2, gate_first * logit_grad, lower), 0.0)
    second_vals = jnp.where(keep, jnp.where(row_of < 2, gate_second * logit_grad, -lower), 0.0)

    def spread(vals, mask, where):
        wide = jnp.broadcast_to(vals[None], (count, 8, tok_rows)).reshape(count * 8, tok_rows)
        high, low = halves(wide * mask)
        return nt(high.astype(BF16), where) + nt(low.astype(BF16), where)

    c_send[...] = (
        spread(first_vals, first_mask, first_at) + spread(second_vals, second_mask, second_at)
    ).reshape(c_send.shape)
    c_start()
    gate_input = jnp.zeros((tok_rows, pooled_ref.shape[1]), F32)
    for task in range(2):
        high, low = halves(signed * first_grad[task : task + 1, :])
        weights = gates[task]
        gate_input += mm(high.astype(BF16), weights, 0, 0) + mm(low.astype(BF16), weights, 0, 0)
    c_wait()
    coefs = jnp.zeros((8, rows_all), F32)
    blank = jnp.zeros((8, rows_all - 128), F32)

    def place(peer, total):
        return total + pltpu.roll(
            jnp.concatenate([c_recv[peer], blank], axis=1), peer * cap, 1
        )

    coefs = lax.fori_loop(0, count, place, coefs)
    coef_zero, coef_one = 0.5 * coefs[0:1, :], 0.5 * coefs[1:2, :]
    back_acc[...] = jnp.zeros_like(back_acc)

    @pl.loop(0, chunks)
    def _(step):
        span = pl.ds(pl.multiple_of(step * chunk, chunk), chunk)
        cols = proj_cols_ref[span, :]
        hidden_grad = cols[:, 0:1] * coef_zero + cols[:, 1:2] * coef_one
        grad = (hidden_grad * slope_ref[span, :]).astype(BF16)
        pre_ref[span, :] = grad
        back_acc[...] += mm(turned_ref[step], grad)

    d_send[...] = back_acc[...].T.astype(BF16).reshape(d_send.shape)
    d_start()

    coef_rows = stacked(coefs)

    def weight_chunk(step, in_target, hidden_target, slot):
        span = pl.ds(pl.multiple_of(step * chunk, chunk), chunk)
        in_target[pl.ds(pl.multiple_of(slot * chunk, chunk), chunk), :] = mm(
            pre_ref[span, :], a_recv[...].reshape(rows_all, -1)
        )
        hidden = folded(nt(coef_rows, act_ref[span, :]))
        hidden_target[slot] = hidden
        return folded(mm(stacked(hidden), out_ref[span, :]))

    tower = jnp.zeros((8, pooled_ref.shape[1]), F32)
    tower = lax.fori_loop(
        0,
        half,
        lambda i, total: total + weight_chunk(other * half + i, in_other, hidden_other, i),
        tower,
    )
    in_copy = to_other(0, in_other, in_recv_hbm)
    hidden_copy = to_other(1, hidden_other, hidden_parts_ref.at[1])
    in_copy.start()
    hidden_copy.start()
    tower = lax.fori_loop(
        0,
        half,
        lambda i, total: total
        + weight_chunk(core * half + i, in_mine, hidden_parts_ref.at[0], i),
        tower,
    )
    gate = folded(mm(coef_rows, a_recv[...].reshape(rows_all, -1)))
    tile = jnp.where(iota(tower.shape, 0) < 2, tower, gate)
    t_send[...] = jnp.broadcast_to(tile[None], t_send.shape)
    t_start()
    store_in = pltpu.make_async_copy(in_mine, in_mine_hbm, local_sem.at[0])
    store_in.start()
    d_wait()
    pooled_grad = gate_input + mm(
        place_ref[...], d_recv[...].reshape(rows_all, -1), 0, 0
    )
    high, low = halves(pooled_grad)
    bag_grad = mm(bag, high.astype(BF16)) + mm(bag, low.astype(BF16))
    e_send[...] = (weight_col * bag_grad).astype(BF16).reshape(e_send.shape)
    e_start()
    r_wait()
    rows_copy = to_other(3, r_recv, rows_ref.at[core])
    rows_copy.start()
    rows_ref[core] = r_recv[...]
    t_wait()
    summed = lax.fori_loop(0, count, lambda i, total: total + t_recv[i], jnp.zeros_like(tower))
    mine = jnp.where(iota(tower.shape, 0) < 2, summed, tile)
    s_send[...] = mine
    small_copy = to_other(4, s_send, s_recv)
    small_copy.start()
    e_wait()
    grads_copy = to_other(2, e_recv, grads_ref.at[core])
    grads_copy.start()
    grads_ref[core] = e_recv[...]
    small_copy.wait()
    small_ref[...] = mine + s_recv[...]
    store_in.wait()
    for copy in (in_copy, hidden_copy, rows_copy, grads_copy):
        copy.wait()
    for drain in (a_drain, b_drain, c_drain, d_drain, e_drain, r_drain, t_drain):
        drain()


def on_device(
    pooled,
    routes,
    labels,
    in_weight,
    out_weight,
    gate_weight,
    tower_weight,
    tower_bias,
    bag_rows,
    bag_sample,
    bag_weight,
    row_table,
):
    count = lax.axis_size("expert")
    tok_rows, feature = pooled.shape
    tasks = tower_weight.shape[0]
    hidden = in_weight.shape[1]
    cap = -(-(3 * tok_rows // count) // 8) * 8
    rows_all = count * cap
    chunk = 1024 if rows_all * 1024 < 2**20 else 512
    chunks = hidden // chunk
    per_owner = bag_rows.shape[0] // count
    held = -(-per_owner // 8) * 8

    def bags(values, empty):
        if held == per_owner:
            return values
        return jnp.pad(
            values.reshape(count, per_owner), ((0, 0), (0, held - per_owner)), constant_values=empty
        )

    vmem = pl.BlockSpec(memory_space=pltpu.VMEM)
    anywhere = pl.BlockSpec(memory_space=pl.ANY)
    scalars = (count, 8, 128)
    routed = (count, cap, feature)
    owned = (count, held, feature)
    half_rows = hidden // 2
    in_mine, in_other, hidden_parts, small, grads, rows = pl.pallas_call(
        functools.partial(kernel, (count, cap, chunk, chunks, per_owner)),
        out_shape=(
            jax.ShapeDtypeStruct((half_rows, feature), F32),
            jax.ShapeDtypeStruct((half_rows, feature), F32),
            jax.ShapeDtypeStruct((2, chunks // 2, 8, chunk), F32),
            jax.ShapeDtypeStruct((8, feature), F32),
            jax.ShapeDtypeStruct((2,) + owned, BF16),
            jax.ShapeDtypeStruct((2,) + scalars, jnp.int32),
        ),
        in_specs=[vmem] * 3
        + [anywhere] * 2
        + [vmem] * 2
        + [pl.BlockSpec(memory_space=pltpu.SMEM)]
        + [vmem] * 3,
        out_specs=(anywhere,) * 2 + (vmem,) * 4,
        scratch_shapes=[
            pltpu.VMEM((hidden, feature), BF16),
            pltpu.VMEM((hidden, feature), BF16),
            pltpu.VMEM((chunks, feature, chunk), BF16),
            pltpu.VMEM((chunks, 16, chunk), BF16),
            pltpu.VMEM((hidden, 8), F32),
            pltpu.VMEM((hidden, rows_all), BF16),
            pltpu.VMEM((hidden, rows_all), F32),
            pltpu.VMEM((hidden, rows_all), BF16),
            pltpu.VMEM((rows_all, tok_rows), BF16),
            pltpu.VMEM(routed, BF16),
            pltpu.VMEM(routed, BF16),
            pltpu.VMEM(scalars, F32),
            pltpu.VMEM(scalars, F32),
            pltpu.VMEM(scalars, F32),
            pltpu.VMEM(scalars, F32),
            pltpu.VMEM(routed, BF16),
            pltpu.VMEM(routed, BF16),
            pltpu.VMEM(owned, BF16),
            pltpu.VMEM(owned, BF16),
            pltpu.VMEM(scalars, jnp.int32),
            pltpu.VMEM(scalars, jnp.int32),
            pltpu.VMEM((count, 8, feature), F32),
            pltpu.VMEM((count, 8, feature), F32),
            pltpu.VMEM((8, feature), F32),
            pltpu.VMEM((8, feature), F32),
            pltpu.VMEM((half_rows, feature), F32),
            pltpu.VMEM((half_rows, feature), F32),
            pltpu.VMEM((chunks // 2, 8, chunk), F32),
            pltpu.VMEM((16, rows_all), F32),
            pltpu.VMEM((feature, rows_all), F32),
            pltpu.SemaphoreType.DMA((7, count)),
            pltpu.SemaphoreType.DMA((7, count)),
            pltpu.SemaphoreType.DMA((5,)),
            pltpu.SemaphoreType.DMA((5,)),
            pltpu.SemaphoreType.DMA((2,)),
        ],
        compiler_params=pltpu.CompilerParams(
            collective_id=0, has_side_effects=True, vmem_limit_bytes=VMEM_LIMIT
        ),
    )(
        pooled,
        routes.T,
        labels.T,
        in_weight[0],
        out_weight[0],
        gate_weight,
        tower_weight,
        tower_bias,
        bag_rows.reshape(-1, 128),
        bags(bag_sample, -1).reshape(1, -1),
        bags(bag_weight, 0.0).reshape(1, -1),
    )
    in_grad = (in_mine + in_other)[None]
    hidden_sum = (hidden_parts[0] + hidden_parts[1])[:, :tasks, :]
    out_grad = sum(
        hidden_sum[:, t].reshape(-1, 1) * tower_weight[t][None, :] for t in range(tasks)
    )[None]
    owned_rows = rows[:, :, 0, :held].reshape(-1)
    matches = (
        jnp.arange(row_table.shape[0], dtype=jnp.int32)[:, None] == owned_rows[None, :]
    ).astype(BF16)
    new_table = row_table - STEP_SIZE * mm(matches, grads.reshape(-1, feature))
    return (in_grad, out_grad, small[None, tasks : 2 * tasks], small[:tasks], new_table)


def solution(mesh):
    in_specs = (
        P(("expert", "dp"), None),
        P(("expert", "dp"), None),
        P(("expert", "dp"), None),
        P("expert", None, None),
        P("expert", None, None),
        P(),
        P(),
        P(),
        P(("expert", "dp")),
        P(("expert", "dp")),
        P(("expert", "dp")),
        P("expert", None),
    )
    out_specs = (
        P("expert", "dp", None),
        P("expert", "dp", None),
        P("expert", None, None),
        P(),
        P("expert", None),
    )
    return jax.shard_map(
        on_device, mesh=mesh, in_specs=in_specs, out_specs=out_specs, check_vma=False
    )
```
